32 devices in a mesh: lat: 8 (over y, x, core), lev: 4 (over z).
Axes of the slice: x: 2, y: 2, z: 4, core: 2. Of those that a mesh axis runs over, the one named last changes fastest.
Arguments:
- tracer: float32 [8, 640, 1280], P('lev', 'lat'), may hold values from -6 to 6
- offsets: int32 [2, 640, 1280], P(None, 'lat'), may hold values from -3 to 3
- stencil: float32 [7, 7], replicated, may hold values from -0.6 to 0.6
- assign: int32 [640], replicated, may hold values from 0 to 639, as said below
- legendre: bfloat16 [640, 2, 320, 320], P('lat', None, 'lev'), may hold values from -0.3125 to 0.3125
- damping: float32 [8], replicated, may hold values from 0.5 to 8
- vert_vecs: float32 [8, 8], replicated, may hold values from -2 to 2
- vert_inv: float32 [8, 8], replicated, may hold values from -2 to 2
Outputs:
- tracer_new: float32 [8, 640, 1280], P('lev', 'lat')
- spectral_new: float32 [640, 2, 320, 16], P('lat', None, 'lev')
The draws below stay inside these ranges and needn't reach their ends.
Inputs may be any that keep to these rules, and one draw needn't show every extreme that they name: `assign`: a permutation of 0 to 639 in which slots 2 u and 2 u + 1 hold the wavenumbers m and 639 - m.
All inputs are finite; a program needn't handle non-finite values.
Results may differ from the reference program's by a relative error of at most 0.0036.
Values may be sent and summed in bfloat16 or wider, within the bound.
A program may use at most 192 MiB of HBM per device.

```python
import math
import jax
import jax.numpy as jnp
from jax import lax

NLON = 1280
NLAT = 640
M = 640
NLEV = 8
HALF_DEG = 320
HALF_LAT = 320


def draw_assign(key, part):
    paired = jax.random.permutation(jax.random.fold_in(key, 7), M // 2).astype(jnp.int32)
    return jnp.stack([paired, M - 1 - paired], axis=1).reshape(M)


def place_ends(result, stream_key, low, largest):
    longest = result.shape.index(max(result.shape))
    spots = []
    for shift in (0, 1):
        where = [jax.random.randint(jax.random.fold_in(stream_key, axis), (), 0, length) for axis, length in enumerate(result.shape)]
        where[longest] = (where[longest] + shift) % result.shape[longest]
        spots.append(tuple(where))
    return result.at[spots[0]].set(low).at[spots[1]].set(largest)


def level_of(key, dims, shards, least, top_value):
    level = 1.0
    for dim, shards_of in shards:
        steps = jax.random.uniform(jax.random.fold_in(jax.random.fold_in(key, 6), dim), (shards_of,), jnp.float32, least / len(shards), top_value / len(shards))
        level = level * jnp.repeat(jnp.exp(steps), dims[dim] // shards_of).reshape((-1,) + (1,) * (len(dims) - 1 - dim))
    return level


def scatter_about(stream_key, shape, deviation, limit, split=(), kind=jnp.bfloat16):
    level = level_of(stream_key, shape, split, -0.22, 0.18) if split else 1.0
    values = jax.random.normal(stream_key, shape, jnp.float32) * deviation * level
    return jnp.minimum(jnp.maximum(values, -limit), limit).astype(kind)


def setup_inputs(seed: int = 0) -> dict:
    streams_of = jax.random.split(jax.random.key(seed), 9)
    tracer = scatter_about(streams_of[0], (NLEV, NLAT, NLON), 1.0, 6.0, ((0, 4), (1, 8)), jnp.float32)
    offsets = place_ends(jax.random.randint(streams_of[1], (2, NLAT, NLON), -3, 4), jax.random.fold_in(streams_of[1], 1), -3, 3).astype(jnp.int32)
    stencil = scatter_about(streams_of[2], (7, 7), 0.15, 0.6, (), jnp.float32)
    assign = draw_assign(jax.random.fold_in(streams_of[8], 71), 0)
    legendre = scatter_about(streams_of[4], (M, 2, HALF_DEG, HALF_LAT), HALF_LAT ** -0.5, 0.3125, ((0, 8), (2, 4)))
    damping = jnp.clip(jnp.exp(jax.random.uniform(streams_of[5], (NLEV,), jnp.float32, math.log(0.5), math.log(8.0))), 0.5, 8.0)
    vert_vecs = scatter_about(streams_of[6], (NLEV, NLEV), NLEV ** -0.5, 2.0, (), jnp.float32)
    vert_inv = scatter_about(streams_of[7], (NLEV, NLEV), NLEV ** -0.5, 2.0, (), jnp.float32)
    return dict(tracer=tracer, offsets=offsets, stencil=stencil, assign=assign, legendre=legendre, damping=damping, vert_vecs=vert_vecs, vert_inv=vert_inv)


EXACT = lax.Precision.HIGHEST

def transport(padded, offsets, stencil):
    row_count = offsets.shape[1]
    summed = jnp.zeros((padded.shape[0], row_count, padded.shape[2]), jnp.float32)
    for row_step in range(-3, 4):
        band_rows = padded[:, 3 + row_step:3 + row_step + row_count, :]
        for col_step in range(-3, 4):
            shifted = jnp.roll(band_rows, -col_step, axis=2)
            picked = jnp.logical_and(offsets[0] == row_step, offsets[1] == col_step).astype(jnp.float32)
            summed = summed + (stencil[row_step + 3, col_step + 3] + picked)[None, :, :] * shifted
    return summed

def wave_angles(assign, lon_cells):
    longitudes = jnp.arange(lon_cells, dtype=jnp.int32)
    phase_index = longitudes[:, None] * assign[None, :].astype(jnp.int32) % lon_cells
    angles = phase_index.astype(jnp.float32) * (2.0 * math.pi / lon_cells)
    return (angles, 1.0 / math.sqrt(lon_cells))

def forward_table(assign, lon_cells):
    angles, norm_scale = wave_angles(assign, lon_cells)
    return jnp.stack([jnp.cos(angles) * norm_scale, -jnp.sin(angles) * norm_scale], axis=2)

def inverse_table(assign, lon_cells):
    angles, norm_scale = wave_angles(assign, lon_cells)
    weights = jnp.where(assign == 0, 1.0, 2.0).astype(jnp.float32) * norm_scale
    cosines = jnp.cos(angles).T * weights[:, None]
    sines = -jnp.sin(angles).T * weights[:, None]
    return jnp.stack([cosines, sines], axis=1)

def split_hemispheres(fourier):
    half_lat = fourier.shape[-1] // 2
    north_half = fourier[..., :half_lat]
    south_half = fourier[..., ::-1][..., :half_lat]
    return jnp.stack([north_half + south_half, north_half - south_half], axis=1).astype(jnp.bfloat16)

def vertical(spectra, my_waves, first_degree, damping, vert_vecs, vert_inv):
    degree_span = spectra.shape[2]
    degrees = first_degree + jnp.arange(degree_span, dtype=jnp.int32)
    parity = jnp.arange(2, dtype=jnp.int32)
    degree_n = my_waves.astype(jnp.int32)[:, None, None] + 2 * degrees[None, None, :] + parity[None, :, None]
    inside = (degree_n <= M - 1).astype(jnp.float32)
    forcing = spectra * inside[:, :, :, None, None]
    modal = jnp.einsum('kq,rpicq->rpick', vert_inv, forcing, precision=EXACT)
    scaled_n = degree_n.astype(jnp.float32)
    growth = scaled_n * (scaled_n + 1.0) / float(M * M)
    denominator = 1.0 + growth[:, :, :, None, None] * damping[None, None, None, None, :]
    modal = modal / denominator
    return jnp.einsum('kq,rpicq->rpick', vert_vecs, modal, precision=EXACT)

def reference(tracer, offsets, stencil, assign, legendre, damping, vert_vecs, vert_inv):
    lon_cells = tracer.shape[2]
    padded = jnp.pad(tracer, ((0, 0), (3, 3), (0, 0)))
    advected = transport(padded, offsets, stencil)
    fourier = jnp.einsum('lij,jrc->rcli', advected, forward_table(assign, lon_cells), precision=EXACT)
    hemispheres = split_hemispheres(fourier)

    def forward_slot(pair):
        table_slot, hemi_slot = pair
        return jnp.einsum('pij,pclj->picl', table_slot.astype(jnp.float32), hemi_slot.astype(jnp.float32))
    spectra = lax.map(forward_slot, (legendre, hemispheres))
    solved = vertical(spectra, assign, 0, damping, vert_vecs, vert_inv)
    packed = solved.astype(jnp.bfloat16)

    def inverse_slot(pair):
        table_slot, packed_slot = pair
        return jnp.einsum('pij,picl->lpcj', table_slot.astype(jnp.float32), packed_slot.astype(jnp.float32))
    back_terms = lax.map(inverse_slot, (legendre, packed))
    north_half = back_terms[:, :, 0] + back_terms[:, :, 1]
    south_half = back_terms[:, :, 0] - back_terms[:, :, 1]
    zonal = jnp.concatenate([north_half, south_half[..., ::-1]], axis=-1)
    tracer_new = jnp.einsum('rlci,rcj->lij', zonal, inverse_table(assign, lon_cells), precision=EXACT)
    spectral_new = solved.reshape(solved.shape[0], 2, solved.shape[2], 2 * solved.shape[4])
    return (tracer_new, spectral_new)
```

```python
import functools
import math

import jax
import jax.numpy as jnp
from jax import lax
from jax.experimental import pallas as pl
from jax.experimental.pallas import tpu as pltpu
from jax.sharding import PartitionSpec as P

M = 640
LANES = 128
REACH = 3

EXACT = lax.Precision.HIGHEST
HIGH = lax.Precision.HIGH


def exchange_kernel(axis, count, spread, x_ref, o_ref, send_sems, recv_sems, own_sem):
    me = lax.axis_index(axis)
    barrier = pltpu.get_barrier_semaphore()
    for step in range(1, count):
        peer = lax.rem(me + step, count)
        pl.semaphore_signal(
            barrier, inc=1, device_id={axis: peer}, device_id_type=pl.DeviceIdType.MESH
        )
    pl.semaphore_wait(barrier, count - 1)
    copies = []
    for step in range(1, count):
        peer = lax.rem(me + step, count)
        copy = pltpu.make_async_remote_copy(
            src_ref=x_ref.at[peer] if spread else x_ref,
            dst_ref=o_ref.at[me],
            send_sem=send_sems.at[step - 1],
            recv_sem=recv_sems.at[step - 1],
            device_id={axis: peer},
            device_id_type=pl.DeviceIdType.MESH,
        )
        copy.start()
        copies.append(copy)
    own = pltpu.make_async_copy(x_ref.at[me] if spread else x_ref, o_ref.at[me], own_sem)
    own.start()
    own.wait()
    for copy in copies:
        copy.wait()


def exchange(x, axis, collective_id, spread=True):
    count = lax.axis_size(axis)
    block = x.shape[1:] if spread else x.shape
    return pl.pallas_call(
        functools.partial(exchange_kernel, axis, count, spread),
        out_shape=jax.ShapeDtypeStruct((count,) + block, x.dtype),
        in_specs=[pl.BlockSpec(memory_space=pltpu.VMEM)],
        out_specs=pl.BlockSpec(memory_space=pltpu.VMEM),
        scratch_shapes=[
            pltpu.SemaphoreType.DMA((count - 1,)),
            pltpu.SemaphoreType.DMA((count - 1,)),
            pltpu.SemaphoreType.DMA,
        ],
        compiler_params=pltpu.CompilerParams(
            collective_id=collective_id, has_side_effects=True
        ),
        name="exchange_%d" % collective_id,
    )(x)


def dense(x):
    size = math.prod(x.shape[1:])
    short = -size % LANES
    flat = x.reshape(x.shape[0], size)
    if short:
        flat = jnp.pad(flat, ((0, 0), (0, short)))
    return flat.reshape(x.shape[0], (size + short) // LANES, LANES)


def loose(x, shape):
    size = math.prod(shape[1:])
    flat = x.reshape(shape[0], x.shape[1] * LANES)
    return flat[:, :size].reshape(shape)


def transport_kernel(stencil_ref, band_ref, up_ref, down_ref, code_ref, o_ref, ext, codes, rolled):
    levels, rows, cells = band_ref.shape
    tall = ext.shape[1]
    codes[...] = jnp.full(codes.shape, -1, jnp.int32)
    codes[0:rows, :] = code_ref[...]
    for level in range(levels):
        ext[level, tall - 8 : tall, :] = jnp.zeros((8, cells), jnp.float32)
        ext[level, 0:REACH, :] = up_ref[level]
        ext[level, REACH : REACH + rows, :] = band_ref[level]
        ext[level, REACH + rows : 2 * REACH + rows, :] = down_ref[level]
        for b in range(7):
            whole = ext[level]
            shift = (REACH - b) % cells
            rolled[b, level] = pltpu.roll(whole, shift, 1) if shift else whole

    @pl.loop(0, cells // LANES)
    def _(column):
        lanes = pl.ds(pl.multiple_of(column * LANES, LANES), LANES)
        code = codes[:, lanes]
        sums = [jnp.zeros((tall, LANES), jnp.float32) for _ in range(levels)]
        for a in range(7):
            code_a = pltpu.roll(code, a, 0) if a else code
            terms = [None] * levels
            for b in range(7):
                weight = stencil_ref[a, b]
                factor = jnp.where(code_a == a * 7 + b, weight + 1.0, weight)
                for level in range(levels):
                    term = factor * rolled[b, level, :, lanes]
                    terms[level] = term if b == 0 else terms[level] + term
            for level in range(levels):
                term = pltpu.roll(terms[level], tall - a, 0) if a else terms[level]
                sums[level] = sums[level] + term
        for level in range(levels):
            o_ref[level, :, lanes] = sums[level][0:rows]


def transport(band, up, down, offsets, stencil):
    levels, rows, cells = band.shape
    tall = -(-(rows + 2 * REACH) // 8) * 8
    code = (offsets[0] + REACH) * 7 + offsets[1] + REACH
    vmem = pl.BlockSpec(memory_space=pltpu.VMEM)
    return pl.pallas_call(
        transport_kernel,
        out_shape=jax.ShapeDtypeStruct(band.shape, jnp.float32),
        in_specs=[pl.BlockSpec(memory_space=pltpu.SMEM), vmem, vmem, vmem, vmem],
        out_specs=vmem,
        scratch_shapes=[
            pltpu.VMEM((levels, tall, cells), jnp.float32),
            pltpu.VMEM((tall, cells), jnp.int32),
            pltpu.VMEM((7, levels, tall, cells), jnp.float32),
        ],
        name="transport",
    )(stencil, band, up, down, code)


def halo(cells, width):
    count = lax.axis_size("lat")
    ends = count - 1
    head = cells[:, :width]
    tail = cells[:, cells.shape[1] - width :]
    up = lax.ppermute(tail, "lat", [(i, i + 1) for i in range(ends)])
    down = lax.ppermute(head, "lat", [(i + 1, i) for i in range(ends)])
    return up, down


def trig(steps, assign, lon_cells):
    phase = steps[:, None] * assign[None, :] % lon_cells
    angles = phase.astype(jnp.float32) * (2.0 * math.pi / lon_cells)
    return jnp.cos(angles), jnp.sin(angles)


def wave_table(assign, lon_cells):
    fine = jnp.arange(LANES, dtype=jnp.int32)
    coarse = jnp.arange(lon_cells // LANES, dtype=jnp.int32) * LANES
    c2, s2 = trig(fine, assign, lon_cells)
    c1, s1 = trig(coarse, assign, lon_cells)
    scale = 1.0 / math.sqrt(lon_cells)
    c1, s1, c2, s2 = lax.optimization_barrier((c1 * scale, s1 * scale, c2, s2))
    cosines = c1[:, None] * c2[None] - s1[:, None] * s2[None]
    sines = -(s1[:, None] * c2[None] + c1[:, None] * s2[None])
    shape = (lon_cells, assign.shape[0])
    return jnp.stack([cosines.reshape(shape), sines.reshape(shape)], axis=1)


def vertical(spectra, my_waves, first_degree, damping, vert_vecs, vert_inv):
    degree_span = spectra.shape[2]
    degrees = first_degree + jnp.arange(degree_span, dtype=jnp.int32)
    parity = jnp.arange(2, dtype=jnp.int32)
    degree_n = my_waves[:, None, None] + 2 * degrees[None, None, :] + parity[None, :, None]
    inside = (degree_n <= M - 1).astype(jnp.float32)
    forcing = spectra * inside[:, :, :, None, None]
    modal = jnp.einsum("kq,rpicq->rpick", vert_inv, forcing, precision=EXACT)
    scaled_n = degree_n.astype(jnp.float32)
    growth = scaled_n * (scaled_n + 1.0) / float(M * M)
    denominator = 1.0 + growth[:, :, :, None, None] * damping[None, None, None, None, :]
    modal = modal / denominator
    return jnp.einsum("kq,rpicq->rpick", vert_vecs, modal, precision=EXACT)


def on_device(tracer, offsets, stencil, assign, legendre, damping, vert_vecs, vert_inv):
    levels, rows, lon_cells = tracer.shape
    bands = lax.axis_size("lat")
    planes = lax.axis_size("lev")
    slots = legendre.shape[0]
    half = bands // 2
    half_lat = half * rows
    me = lax.axis_index("lat")
    southern = me >= half

    up, down = halo(tracer, REACH)
    table = wave_table(assign, lon_cells)
    advected = transport(tracer, up, down, offsets, stencil)
    advected = jnp.where(southern, advected[:, ::-1], advected)
    fourier = jnp.einsum("lij,jcr->rcli", advected, table, precision=HIGH)
    sent = fourier.reshape(bands, slots, 2, levels, rows)
    got = loose(exchange(dense(sent), "lat", 1), (bands, slots, 2, levels, rows))
    north = got[:half]
    south = got[half:][::-1]
    hemi = jnp.stack([north + south, north - south], axis=1)
    hemi = hemi.transpose(2, 1, 3, 4, 0, 5).reshape(1, -1).astype(jnp.bfloat16)
    hemi = exchange(dense(hemi)[0], "lev", 2, spread=False)
    hemi = loose(hemi, (planes, slots, 2, 2, levels, half_lat))
    hemi = hemi.transpose(1, 2, 3, 0, 4, 5).reshape(slots, 2, 2, planes * levels, half_lat)

    my_waves = lax.dynamic_slice_in_dim(assign, me * slots, slots)
    first_degree = lax.axis_index("lev") * legendre.shape[2]
    spectra = jnp.einsum(
        "rpij,rpclj->rpicl", legendre, hemi, preferred_element_type=jnp.float32
    )
    solved = vertical(spectra, my_waves, first_degree, damping, vert_vecs, vert_inv)
    packed = solved.astype(jnp.bfloat16)
    back = jnp.einsum(
        "rpij,rpicl->rpclj", legendre, packed, preferred_element_type=jnp.float32
    )
    back = back.astype(jnp.bfloat16).reshape(slots, 2, 2, planes, levels, half_lat)
    parts = exchange(dense(back.transpose(3, 0, 1, 2, 4, 5)), "lev", 3)
    parts = loose(parts, (planes, slots, 2, 2, levels, half, rows))
    total = jnp.sum(parts.astype(jnp.float32), axis=0)
    even, odd = total[:, 0], total[:, 1]
    zonal = jnp.concatenate([even + odd, (even - odd)[:, :, :, ::-1]], axis=3)
    zonal = zonal.transpose(3, 0, 1, 2, 4).astype(jnp.bfloat16)
    waves = loose(exchange(dense(zonal), "lat", 4), (bands, slots, 2, levels, rows))
    waves = waves.reshape(bands * slots, 2, levels, rows)
    weights = jnp.where(assign == 0, 1.0, 2.0).astype(jnp.float32)
    waves = waves.astype(jnp.float32) * weights[:, None, None, None]
    tracer_new = jnp.einsum("rcli,jcr->lij", waves, table, precision=HIGH)
    tracer_new = jnp.where(southern, tracer_new[:, ::-1], tracer_new)
    spectral_new = solved.reshape(slots, 2, solved.shape[2], -1)
    return (tracer_new, spectral_new)


def solution(mesh):
    in_specs = (
        P("lev", "lat", None),
        P(None, "lat", None),
        P(),
        P(),
        P("lat", None, "lev", None),
        P(),
        P(),
        P(),
    )
    out_specs = (P("lev", "lat", None), P("lat", None, "lev", None))
    return jax.shard_map(
        on_device, mesh=mesh, in_specs=in_specs, out_specs=out_specs, check_vma=False
    )
```

```python
import functools
import math

import jax
import jax.numpy as jnp
from jax import lax
from jax.experimental import pallas as pl
from jax.experimental.pallas import tpu as pltpu
from jax.sharding import PartitionSpec as P

M = 640
LANES = 128
REACH = 3

EXACT = lax.Precision.HIGHEST


def exchange_kernel(axis, count, spread, x_ref, o_ref, send_sems, recv_sems, own_sem):
    me = lax.axis_index(axis)
    barrier = pltpu.get_barrier_semaphore()
    for step in range(1, count):
        peer = lax.rem(me + step, count)
        pl.semaphore_signal(
            barrier, inc=1, device_id={axis: peer}, device_id_type=pl.DeviceIdType.MESH
        )
    pl.semaphore_wait(barrier, count - 1)
    copies = []
    for step in range(1, count):
        peer = lax.rem(me + step, count)
        copy = pltpu.make_async_remote_copy(
            src_ref=x_ref.at[peer] if spread else x_ref,
            dst_ref=o_ref.at[me],
            send_sem=send_sems.at[step - 1],
            recv_sem=recv_sems.at[step - 1],
            device_id={axis: peer},
            device_id_type=pl.DeviceIdType.MESH,
        )
        copy.start()
        copies.append(copy)
    own = pltpu.make_async_copy(x_ref.at[me] if spread else x_ref, o_ref.at[me], own_sem)
    own.start()
    own.wait()
    for copy in copies:
        copy.wait()


def exchange(x, axis, collective_id, spread=True):
    count = lax.axis_size(axis)
    block = x.shape[1:] if spread else x.shape
    return pl.pallas_call(
        functools.partial(exchange_kernel, axis, count, spread),
        out_shape=jax.ShapeDtypeStruct((count,) + block, x.dtype),
        in_specs=[pl.BlockSpec(memory_space=pltpu.VMEM)],
        out_specs=pl.BlockSpec(memory_space=pltpu.VMEM),
        scratch_shapes=[
            pltpu.SemaphoreType.DMA((count - 1,)),
            pltpu.SemaphoreType.DMA((count - 1,)),
            pltpu.SemaphoreType.DMA,
        ],
        compiler_params=pltpu.CompilerParams(
            collective_id=collective_id, has_side_effects=True
        ),
        name="exchange_%d" % collective_id,
    )(x)


def tail_of(wide):
    tail = max(wide - LANES, 0)
    assert tail == 0 or LANES % tail == 0
    return tail


def packed_rows(slots, wide):
    tail = tail_of(wide)
    return 2 * slots + (2 * slots * tail) // LANES


def placement(source, rows, half_lat, band, flip):
    level = jnp.zeros_like(source)
    for k in range(1, 2 + (LANES * 2) // rows):
        level = level + (source >= k * rows).astype(jnp.int32)
    row = source - level * rows
    if flip:
        row = rows - 1 - row
    return level * half_lat + band * rows + row


def one_hot(pick):
    return jnp.where(pick, 1.0, 0.0).astype(jnp.bfloat16)


def split(x):
    high = x.astype(jnp.bfloat16)
    return high, (x - high.astype(jnp.float32)).astype(jnp.bfloat16)


def dot_nt(a, b):
    return lax.dot_general(a, b, (((1,), (1,)), ((), ())), preferred_element_type=jnp.float32)


def dot_nn(a, b):
    return jnp.dot(a, b, preferred_element_type=jnp.float32)


def fill_tables(c1, s1, c2, s2, tables):
    fine_c, fine_s = c2[0], s2[0]
    for a in range(c1.shape[2]):
        lanes = slice(a * LANES, (a + 1) * LANES)
        coarse_c, coarse_s = c1[0, :, a : a + 1], s1[0, :, a : a + 1]
        cosines = coarse_c * fine_c - coarse_s * fine_s
        sines = -(coarse_s * fine_c + coarse_c * fine_s)
        for part, values in enumerate((cosines, sines)):
            high, low = split(values)
            tables[2 * part, :, lanes] = high
            tables[2 * part + 1, :, lanes] = low


def forward_kernel(half, levels, c1, s1, c2, s2, field, o_ref, cells, tables):
    wide = field.shape[0]
    rows = wide // levels
    slots = c1.shape[1]
    padded = cells.shape[1]
    tail = tail_of(wide)
    southern = lax.axis_index("lat") >= half

    @pl.when(pl.program_id(0) == 0)
    def _():
        to = lax.broadcasted_iota(jnp.int32, (padded, wide), 0)
        origin = lax.broadcasted_iota(jnp.int32, (padded, wide), 1)
        level = jnp.zeros_like(to)
        for k in range(1, levels):
            level = level + (to >= k * rows).astype(jnp.int32)
        mirrored = 2 * level * rows + rows - 1 - to
        wanted = jnp.where(southern, mirrored, to)
        pick = one_hot(jnp.logical_and(origin == wanted, to < wide))
        high, low = split(field[...])
        cells[0] = dot_nn(pick, high).astype(jnp.bfloat16)
        cells[1] = dot_nn(pick, low).astype(jnp.bfloat16)

    fill_tables(c1, s1, c2, s2, tables)
    tails = []
    for part in range(2):
        found = (
            dot_nt(tables[2 * part], cells[0])
            + dot_nt(tables[2 * part], cells[1])
            + dot_nt(tables[2 * part + 1], cells[0])
        )
        o_ref[0, part * slots : (part + 1) * slots, :] = found[:, :LANES]
        if tail:
            tails.append(found[:, LANES:])
    if tail:
        groups = LANES // tail
        each = 2 * slots // groups
        both = jnp.concatenate(tails, axis=0)
        total = both[:each]
        for k in range(1, groups):
            total = total + pltpu.roll(both[k * each : (k + 1) * each], k * tail, 1)
        o_ref[0, 2 * slots :, :] = total


def forward(field, levels, trigs, bands, slots):
    wide, cells = field.shape
    padded = LANES * (1 if wide <= LANES else 2)
    rows = packed_rows(slots, wide)
    whole = pl.BlockSpec(field.shape, lambda g: (0, 0))
    per_slot = [pl.BlockSpec((1, slots, t.shape[2]), lambda g: (g, 0, 0)) for t in trigs]
    return pl.pallas_call(
        functools.partial(forward_kernel, bands // 2, levels),
        out_shape=jax.ShapeDtypeStruct((bands, rows, LANES), jnp.float32),
        grid=(bands,),
        in_specs=per_slot + [whole],
        out_specs=pl.BlockSpec((1, rows, LANES), lambda g: (g, 0, 0)),
        scratch_shapes=[
            pltpu.VMEM((2, padded, cells), jnp.bfloat16),
            pltpu.VMEM((4, slots, cells), jnp.bfloat16),
        ],
        name="forward",
    )(*trigs, field)


def hemi_kernel(slots, levels, rows, x_ref, o_ref):
    bands = x_ref.shape[0]
    half = bands // 2
    half_lat = half * rows
    wide = levels * rows
    tail = tail_of(wide)
    length = levels * half_lat
    source = lax.broadcasted_iota(jnp.int32, (LANES, length), 0)
    target = lax.broadcasted_iota(jnp.int32, (LANES, length), 1)
    sums = [None, None]
    for band in range(half):
        north = x_ref[band]
        south = x_ref[bands - 1 - band]
        main = placement(source, rows, half_lat, band, False)
        main = one_hot(jnp.logical_and(target == main, source < wide))
        ends = []
        if tail:
            groups = LANES // tail
            each = 2 * slots // groups
            for k in range(groups):
                cell = source - k * tail + LANES
                lane = placement(cell, rows, half_lat, band, False)
                inside = jnp.logical_and(source >= k * tail, source < (k + 1) * tail)
                ends.append(one_hot(jnp.logical_and(target == lane, inside)))
        for parity, value in enumerate((north + south, north - south)):
            term = dot_nn(value[: 2 * slots].astype(jnp.bfloat16), main)
            if tail:
                end = value[2 * slots :].astype(jnp.bfloat16)
                term = term + jnp.concatenate([dot_nn(end, place) for place in ends], axis=0)
            sums[parity] = term if band == 0 else sums[parity] + term
    for parity in range(2):
        o_ref[parity] = sums[parity].astype(jnp.bfloat16)


def hemispheres(x, slots, levels, rows):
    length = levels * rows * x.shape[0] // 2
    vmem = pl.BlockSpec(memory_space=pltpu.VMEM)
    return pl.pallas_call(
        functools.partial(hemi_kernel, slots, levels, rows),
        out_shape=jax.ShapeDtypeStruct((2, 2 * slots, length), jnp.bfloat16),
        in_specs=[vmem],
        out_specs=vmem,
        name="hemispheres",
    )(x)


def zonal_kernel(slots, levels, rows, x_ref, o_ref):
    planes = x_ref.shape[0]
    bands = o_ref.shape[0]
    half = bands // 2
    half_lat = half * rows
    wide = levels * rows
    tail = tail_of(wide)
    length = levels * half_lat
    totals = []
    for parity in range(2):
        total = x_ref[0, parity].astype(jnp.float32)
        for plane in range(1, planes):
            total = total + x_ref[plane, parity].astype(jnp.float32)
        totals.append(total)
    sides = (totals[0] + totals[1], totals[0] - totals[1])
    source = lax.broadcasted_iota(jnp.int32, (LANES, length), 0)
    target = lax.broadcasted_iota(jnp.int32, (LANES, length), 1)
    for side, value in enumerate(sides):
        flip = side == 1
        groups = LANES // tail if tail else 1
        each = 2 * slots // groups
        whole = value.astype(jnp.bfloat16)
        chunks = [value[k * each : (k + 1) * each].astype(jnp.bfloat16) for k in range(groups)]
        for band in range(half):
            slot = bands - 1 - band if flip else band
            main = placement(source, rows, half_lat, band, flip)
            main = one_hot(jnp.logical_and(target == main, source < wide))
            o_ref[slot, : 2 * slots, :] = dot_nt(whole, main).astype(jnp.bfloat16)
            if tail:
                total = None
                for k in range(groups):
                    cell = source - k * tail + LANES
                    lane = placement(cell, rows, half_lat, band, flip)
                    inside = jnp.logical_and(source >= k * tail, source < (k + 1) * tail)
                    term = dot_nt(chunks[k], one_hot(jnp.logical_and(target == lane, inside)))
                    total = term if k == 0 else total + term
                o_ref[slot, 2 * slots :, :] = total.astype(jnp.bfloat16)


def zonals(x, slots, levels, rows, bands):
    out_rows = packed_rows(slots, levels * rows)
    vmem = pl.BlockSpec(memory_space=pltpu.VMEM)
    return pl.pallas_call(
        functools.partial(zonal_kernel, slots, levels, rows),
        out_shape=jax.ShapeDtypeStruct((bands, out_rows, LANES), jnp.bfloat16),
        in_specs=[vmem],
        out_specs=vmem,
        name="zonals",
    )(x)


def inverse_kernel(c1, s1, c2, s2, x_ref, o_ref, tables):
    wide = o_ref.shape[0]
    slots = c1.shape[1]
    tail = tail_of(wide)
    fill_tables(c1, s1, c2, s2, tables)
    value = x_ref[0].astype(jnp.float32)
    main = value[: 2 * slots]
    pieces = [main]
    if tail:
        groups = LANES // tail
        end = value[2 * slots :]
        spread = [end] + [pltpu.roll(end, LANES - k * tail, 1) for k in range(1, groups)]
        pieces.append(jnp.concatenate(spread, axis=0))
    first = pl.program_id(0) == 0
    for number, piece in enumerate(pieces):
        term = None
        for part in range(2):
            turned = piece[part * slots : (part + 1) * slots].T.astype(jnp.bfloat16)
            for low in range(2):
                one = dot_nn(turned, tables[2 * part + low])
                term = one if term is None else term + one
        begin = number * LANES
        count = min(LANES, wide - begin)
        place = slice(begin, begin + count)

        @pl.when(first)
        def _():
            o_ref[place, :] = term[:count]

        @pl.when(jnp.logical_not(first))
        def _():
            o_ref[place, :] += term[:count]


def inverse(x, trigs, wide, cells):
    bands, rows, _ = x.shape
    slots = trigs[0].shape[1]
    per_slot = [pl.BlockSpec((1, slots, t.shape[2]), lambda g: (g, 0, 0)) for t in trigs]
    return pl.pallas_call(
        inverse_kernel,
        out_shape=jax.ShapeDtypeStruct((wide, cells), jnp.float32),
        grid=(bands,),
        in_specs=per_slot + [pl.BlockSpec((1, rows, LANES), lambda g: (g, 0, 0))],
        out_specs=pl.BlockSpec((wide, cells), lambda g: (0, 0)),
        scratch_shapes=[pltpu.VMEM((4, slots, cells), jnp.bfloat16)],
        name="inverse",
    )(*trigs, x)


def transport_kernel(stencil_ref, band_ref, up_ref, down_ref, code_ref, o_ref, ext, codes, rolled):
    levels, rows, cells = band_ref.shape
    tall = ext.shape[1]
    codes[...] = jnp.full(codes.shape, -1, jnp.int32)
    codes[0:rows, :] = code_ref[...]
    for level in range(levels):
        ext[level, tall - 8 : tall, :] = jnp.zeros((8, cells), jnp.float32)
        ext[level, 0:REACH, :] = up_ref[level]
        ext[level, REACH : REACH + rows, :] = band_ref[level]
        ext[level, REACH + rows : 2 * REACH + rows, :] = down_ref[level]
        for b in range(7):
            whole = ext[level]
            shift = (REACH - b) % cells
            rolled[b, level] = pltpu.roll(whole, shift, 1) if shift else whole

    @pl.loop(0, cells // LANES)
    def _(column):
        lanes = pl.ds(pl.multiple_of(column * LANES, LANES), LANES)
        code = codes[:, lanes]
        sums = [jnp.zeros((tall, LANES), jnp.float32) for _ in range(levels)]
        for a in range(7):
            code_a = pltpu.roll(code, a, 0) if a else code
            terms = [None] * levels
            for b in range(7):
                weight = stencil_ref[a, b]
                factor = jnp.where(code_a == a * 7 + b, weight + 1.0, weight)
                for level in range(levels):
                    term = factor * rolled[b, level, :, lanes]
                    terms[level] = term if b == 0 else terms[level] + term
            for level in range(levels):
                term = pltpu.roll(terms[level], tall - a, 0) if a else terms[level]
                sums[level] = sums[level] + term
        for level in range(levels):
            o_ref[level * rows : (level + 1) * rows, lanes] = sums[level][0:rows]


def transport(band, up, down, offsets, stencil):
    levels, rows, cells = band.shape
    tall = -(-(rows + 2 * REACH) // 8) * 8
    code = (offsets[0] + REACH) * 7 + offsets[1] + REACH
    vmem = pl.BlockSpec(memory_space=pltpu.VMEM)
    return pl.pallas_call(
        transport_kernel,
        out_shape=jax.ShapeDtypeStruct((levels * rows, cells), jnp.float32),
        in_specs=[pl.BlockSpec(memory_space=pltpu.SMEM), vmem, vmem, vmem, vmem],
        out_specs=vmem,
        scratch_shapes=[
            pltpu.VMEM((levels, tall, cells), jnp.float32),
            pltpu.VMEM((tall, cells), jnp.int32),
            pltpu.VMEM((7, levels, tall, cells), jnp.float32),
        ],
        name="transport",
    )(stencil, band, up, down, code)


def halo(cells, width):
    count = lax.axis_size("lat")
    ends = count - 1
    head = cells[:, :width]
    tail = cells[:, cells.shape[1] - width :]
    up = lax.ppermute(tail, "lat", [(i, i + 1) for i in range(ends)])
    down = lax.ppermute(head, "lat", [(i + 1, i) for i in range(ends)])
    return up, down


def trig(steps, assign, lon_cells):
    phase = assign[..., None] * steps % lon_cells
    angles = phase.astype(jnp.float32) * (2.0 * math.pi / lon_cells)
    return jnp.cos(angles), jnp.sin(angles)


def wave_trigs(assign, lon_cells):
    fine = jnp.arange(LANES, dtype=jnp.int32)
    coarse = jnp.arange(lon_cells // LANES, dtype=jnp.int32) * LANES
    c2, s2 = trig(fine, assign, lon_cells)
    c1, s1 = trig(coarse, assign, lon_cells)
    scale = 1.0 / math.sqrt(lon_cells)
    weights = jnp.where(assign == 0, 1.0, 2.0)
    weights = weights.astype(jnp.float32)[..., None]
    c1, s1 = c1 * scale, s1 * scale
    return (c1, s1, c2, s2), (c1 * weights, s1 * weights, c2, s2)


def vertical(spectra, my_waves, first_degree, damping, vert_vecs, vert_inv):
    degree_span = spectra.shape[2]
    degrees = first_degree + jnp.arange(degree_span, dtype=jnp.int32)
    parity = jnp.arange(2, dtype=jnp.int32)
    degree_n = my_waves[:, None, None] + 2 * degrees[None, None, :] + parity[None, :, None]
    inside = (degree_n <= M - 1).astype(jnp.float32)
    forcing = spectra * inside[:, :, :, None, None]
    modal = jnp.einsum("kq,rpicq->rpick", vert_inv, forcing, precision=EXACT)
    scaled_n = degree_n.astype(jnp.float32)
    growth = scaled_n * (scaled_n + 1.0) / float(M * M)
    denominator = 1.0 + growth[:, :, :, None, None] * damping[None, None, None, None, :]
    modal = modal / denominator
    return jnp.einsum("kq,rpicq->rpick", vert_vecs, modal, precision=EXACT)


def on_device(tracer, offsets, stencil, assign, legendre, damping, vert_vecs, vert_inv):
    levels, rows, lon_cells = tracer.shape
    bands = lax.axis_size("lat")
    planes = lax.axis_size("lev")
    slots = legendre.shape[0]
    half = bands // 2
    half_lat = half * rows
    me = lax.axis_index("lat")
    up, down = halo(tracer, REACH)
    to_waves, from_waves = wave_trigs(assign.reshape(bands, slots), lon_cells)
    advected = transport(tracer, up, down, offsets, stencil)
    sent = forward(advected, levels, to_waves, bands, slots)
    got = exchange(sent, "lat", 1)
    hemi = exchange(hemispheres(got, slots, levels, rows), "lev", 2, spread=False)
    hemi = hemi.reshape(planes, 2, 2, slots, levels, half_lat)
    hemi = hemi.transpose(3, 1, 2, 0, 4, 5).reshape(slots, 2, 2, planes * levels, half_lat)

    my_waves = lax.dynamic_slice_in_dim(assign, me * slots, slots)
    first_degree = lax.axis_index("lev") * legendre.shape[2]
    spectra = jnp.einsum(
        "rpij,rpclj->rpicl", legendre, hemi, preferred_element_type=jnp.float32
    )
    solved = vertical(spectra, my_waves, first_degree, damping, vert_vecs, vert_inv)
    packed = solved.astype(jnp.bfloat16)
    back = jnp.einsum(
        "rpij,rpicl->rpclj", legendre, packed, preferred_element_type=jnp.float32
    )
    back = back.astype(jnp.bfloat16).reshape(slots, 2, 2, planes, levels, half_lat)
    back = back.transpose(3, 1, 2, 0, 4, 5).reshape(planes, 2, 2 * slots, levels * half_lat)
    parts = exchange(back, "lev", 3)
    waves = exchange(zonals(parts, slots, levels, rows, bands), "lat", 4)
    tracer_new = inverse(waves, from_waves, levels * rows, lon_cells)
    tracer_new = tracer_new.reshape(levels, rows, lon_cells)
    spectral_new = solved.reshape(slots, 2, solved.shape[2], -1)
    return (tracer_new, spectral_new)


def solution(mesh):
    in_specs = (
        P("lev", "lat", None),
        P(None, "lat", None),
        P(),
        P(),
        P("lat", None, "lev", None),
        P(),
        P(),
        P(),
    )
    out_specs = (P("lev", "lat", None), P("lat", None, "lev", None))
    return jax.shard_map(
        on_device, mesh=mesh, in_specs=in_specs, out_specs=out_specs, check_vma=False
    )
```

```python
import functools
import math

import jax
import jax.numpy as jnp
from jax import lax
from jax.experimental import pallas as pl
from jax.experimental.pallas import tpu as pltpu
from jax.sharding import PartitionSpec as P

M = 640
LANES = 128
REACH = 3

EXACT = lax.Precision.HIGHEST


def exchange_kernel(axis, count, x_ref, o_ref, send_sems, recv_sems, own_sem):
    me = lax.axis_index(axis)
    barrier = pltpu.get_barrier_semaphore()
    for step in range(1, count):
        peer = lax.rem(me + step, count)
        pl.semaphore_signal(
            barrier, inc=1, device_id={axis: peer}, device_id_type=pl.DeviceIdType.MESH
        )
    pl.semaphore_wait(barrier, count - 1)
    copies = []
    for step in range(1, count):
        peer = lax.rem(me + step, count)
        copy = pltpu.make_async_remote_copy(
            src_ref=x_ref.at[peer],
            dst_ref=o_ref.at[me],
            send_sem=send_sems.at[step - 1],
            recv_sem=recv_sems.at[step - 1],
            device_id={axis: peer},
            device_id_type=pl.DeviceIdType.MESH,
        )
        copy.start()
        copies.append(copy)
    own = pltpu.make_async_copy(x_ref.at[me], o_ref.at[me], own_sem)
    own.start()
    own.wait()
    for copy in copies:
        copy.wait()


def exchange(x, axis, collective_id):
    count = lax.axis_size(axis)
    return pl.pallas_call(
        functools.partial(exchange_kernel, axis, count),
        out_shape=jax.ShapeDtypeStruct(x.shape, x.dtype),
        in_specs=[pl.BlockSpec(memory_space=pltpu.VMEM)],
        out_specs=pl.BlockSpec(memory_space=pltpu.VMEM),
        scratch_shapes=[
            pltpu.SemaphoreType.DMA((count - 1,)),
            pltpu.SemaphoreType.DMA((count - 1,)),
            pltpu.SemaphoreType.DMA,
        ],
        compiler_params=pltpu.CompilerParams(
            collective_id=collective_id, has_side_effects=True
        ),
        name="exchange_%d" % collective_id,
    )(x)


def greet_neighbours(axis, count, me):
    barrier = pltpu.get_barrier_semaphore()
    ways = ((me > 0, me - 1), (me < count - 1, me + 1))
    for there, peer in ways:

        @pl.when(there)
        def _():
            pl.semaphore_signal(
                barrier, inc=1, device_id={axis: peer}, device_id_type=pl.DeviceIdType.MESH
            )

    inner = jnp.logical_and(me > 0, me < count - 1)

    @pl.when(inner)
    def _():
        pl.semaphore_wait(barrier, 2)

    @pl.when(jnp.logical_not(inner))
    def _():
        pl.semaphore_wait(barrier, 1)


def gather_kernel(axis, count, x_ref, o_ref, send_sems, recv_sems, own_sem):
    me = lax.axis_index(axis)
    greet_neighbours(axis, count, me)
    own = pltpu.make_async_copy(x_ref, o_ref.at[me], own_sem)
    own.start()

    def hop(way, k):
        sign = 1 - 2 * way
        block, target = me + sign * k, me - sign
        held = jnp.logical_and(block >= 0, block < count)
        onward = jnp.logical_and(held, jnp.logical_and(target >= 0, target < count))
        copy = pltpu.make_async_remote_copy(
            src_ref=o_ref.at[block] if k else x_ref,
            dst_ref=o_ref.at[block],
            send_sem=send_sems.at[way, k],
            recv_sem=recv_sems.at[way, k],
            device_id={axis: target},
            device_id_type=pl.DeviceIdType.MESH,
        )
        return held, onward, copy

    def landed(way, k):
        block = me + (1 - 2 * way) * k
        return pltpu.make_async_remote_copy(
            src_ref=x_ref,
            dst_ref=o_ref.at[block],
            send_sem=send_sems.at[way, k - 1],
            recv_sem=recv_sems.at[way, k - 1],
            device_id={axis: lax.rem(me + 1, count)},
            device_id_type=pl.DeviceIdType.MESH,
        )

    for k in range(count):
        for way in range(2):
            held, onward, copy = hop(way, k)
            if k:

                @pl.when(held)
                def _():
                    landed(way, k).wait_recv()

            if k < count - 1:

                @pl.when(onward)
                def _():
                    copy.start()

    own.wait()
    for k in range(count - 1):
        for way in range(2):
            held, onward, copy = hop(way, k)

            @pl.when(onward)
            def _():
                copy.wait_send()


def gather(x, axis, collective_id):
    count = lax.axis_size(axis)
    return pl.pallas_call(
        functools.partial(gather_kernel, axis, count),
        out_shape=jax.ShapeDtypeStruct((count,) + x.shape, x.dtype),
        in_specs=[pl.BlockSpec(memory_space=pltpu.VMEM)],
        out_specs=pl.BlockSpec(memory_space=pltpu.VMEM),
        scratch_shapes=[
            pltpu.SemaphoreType.DMA((2, count)),
            pltpu.SemaphoreType.DMA((2, count)),
            pltpu.SemaphoreType.DMA,
        ],
        compiler_params=pltpu.CompilerParams(
            collective_id=collective_id, has_side_effects=True
        ),
        name="gather_%d" % collective_id,
    )(x)


def scatter_kernel(axis, count, x_ref, o_ref, land, outs, send_sems, recv_sems):
    me = lax.axis_index(axis)
    greet_neighbours(axis, count, me)
    fed_from = (me < count - 1, me > 0)
    parities = x_ref.shape[1]

    def leg(way, dest, source, target):
        return pltpu.make_async_remote_copy(
            src_ref=source,
            dst_ref=land.at[way, dest],
            send_sem=send_sems.at[way, dest],
            recv_sem=recv_sems.at[way, dest],
            device_id={axis: target},
            device_id_type=pl.DeviceIdType.MESH,
        )

    legs = []
    for k in range(count - 1):
        for way in range(2):
            dest = k if way == 0 else count - 1 - k
            away = me > dest if way == 0 else me < dest
            target = me - 1 if way == 0 else me + 1
            legs.append((way, dest, away, target))

            @pl.when(jnp.logical_and(away, jnp.logical_not(fed_from[way])))
            def _():
                leg(way, dest, x_ref.at[dest], target).start()

            @pl.when(jnp.logical_and(away, fed_from[way]))
            def _():
                leg(way, dest, x_ref.at[dest], target).wait_recv()

                @pl.loop(0, parities)
                def _(parity):
                    total = land[way, dest, parity].astype(jnp.float32)
                    total = total + x_ref[dest, parity].astype(jnp.float32)
                    outs[way, dest, parity] = total.astype(outs.dtype)

                leg(way, dest, outs.at[way, dest], target).start()

    @pl.loop(0, parities)
    def _(parity):
        o_ref[parity] = x_ref[me, parity].astype(jnp.float32)

    for way in range(2):

        @pl.when(fed_from[way])
        def _():
            leg(way, me, x_ref.at[me], lax.rem(me + 1, count)).wait_recv()

            @pl.loop(0, parities)
            def _(parity):
                o_ref[parity] += land[way, me, parity].astype(jnp.float32)

    for way, dest, away, target in legs:

        @pl.when(away)
        def _():
            leg(way, dest, outs.at[way, dest], target).wait_send()


def scatter(x, axis, collective_id):
    count = lax.axis_size(axis)
    vmem = pl.BlockSpec(memory_space=pltpu.VMEM)
    return pl.pallas_call(
        functools.partial(scatter_kernel, axis, count),
        out_shape=jax.ShapeDtypeStruct(x.shape[1:], jnp.float32),
        in_specs=[vmem],
        out_specs=vmem,
        scratch_shapes=[
            pltpu.VMEM((2,) + x.shape, x.dtype),
            pltpu.VMEM((2,) + x.shape, x.dtype),
            pltpu.SemaphoreType.DMA((2, count)),
            pltpu.SemaphoreType.DMA((2, count)),
        ],
        compiler_params=pltpu.CompilerParams(
            collective_id=collective_id, has_side_effects=True
        ),
        name="scatter_%d" % collective_id,
    )(x)


def tail_of(wide):
    tail = max(wide - LANES, 0)
    assert tail == 0 or LANES % tail == 0
    return tail


def packed_rows(slots, wide):
    tail = tail_of(wide)
    return 2 * slots + (2 * slots * tail) // LANES


def placement(source, rows, half_lat, band, flip):
    level = jnp.zeros_like(source)
    for k in range(1, 2 + (LANES * 2) // rows):
        level = level + (source >= k * rows).astype(jnp.int32)
    row = source - level * rows
    if flip:
        row = rows - 1 - row
    return level * half_lat + band * rows + row


def one_hot(pick):
    return jnp.where(pick, 1.0, 0.0).astype(jnp.bfloat16)


def split(x):
    high = x.astype(jnp.bfloat16)
    return high, (x - high.astype(jnp.float32)).astype(jnp.bfloat16)


def dot_nt(a, b):
    return lax.dot_general(a, b, (((1,), (1,)), ((), ())), preferred_element_type=jnp.float32)


def dot_nn(a, b):
    return jnp.dot(a, b, preferred_element_type=jnp.float32)


def fill_tables(c1, s1, c2, s2, tables):
    fine_c, fine_s = c2[0], s2[0]
    for a in range(c1.shape[2]):
        lanes = slice(a * LANES, (a + 1) * LANES)
        coarse_c, coarse_s = c1[0, :, a : a + 1], s1[0, :, a : a + 1]
        cosines = coarse_c * fine_c - coarse_s * fine_s
        sines = -(coarse_s * fine_c + coarse_c * fine_s)
        for part, values in enumerate((cosines, sines)):
            high, low = split(values)
            tables[0, 2 * part, :, lanes] = high
            tables[0, 2 * part + 1, :, lanes] = low


def forward_kernel(half, levels, c1, s1, c2, s2, field, o_ref, tables, cells):
    wide = field.shape[0]
    rows = wide // levels
    slots = c1.shape[1]
    padded = cells.shape[1]
    tail = tail_of(wide)
    southern = lax.axis_index("lat") >= half

    @pl.when(pl.program_id(0) == 0)
    def _():
        to = lax.broadcasted_iota(jnp.int32, (padded, wide), 0)
        origin = lax.broadcasted_iota(jnp.int32, (padded, wide), 1)
        level = jnp.zeros_like(to)
        for k in range(1, levels):
            level = level + (to >= k * rows).astype(jnp.int32)
        mirrored = 2 * level * rows + rows - 1 - to
        wanted = jnp.where(southern, mirrored, to)
        pick = one_hot(jnp.logical_and(origin == wanted, to < wide))
        high, low = split(field[...])
        cells[0] = dot_nn(pick, high).astype(jnp.bfloat16)
        cells[1] = dot_nn(pick, low).astype(jnp.bfloat16)

    fill_tables(c1, s1, c2, s2, tables)
    tails = []
    for part in range(2):
        found = (
            dot_nt(tables[0, 2 * part], cells[0])
            + dot_nt(tables[0, 2 * part], cells[1])
            + dot_nt(tables[0, 2 * part + 1], cells[0])
        )
        o_ref[0, part * slots : (part + 1) * slots, :] = found[:, :LANES]
        if tail:
            tails.append(found[:, LANES:])
    if tail:
        groups = LANES // tail
        each = 2 * slots // groups
        both = jnp.concatenate(tails, axis=0)
        total = both[:each]
        for k in range(1, groups):
            total = total + pltpu.roll(both[k * each : (k + 1) * each], k * tail, 1)
        o_ref[0, 2 * slots :, :] = total


def forward(field, levels, trigs, bands, slots):
    wide, cells = field.shape
    padded = LANES * (1 if wide <= LANES else 2)
    rows = packed_rows(slots, wide)
    whole = pl.BlockSpec(field.shape, lambda g: (0, 0))
    per_slot = [pl.BlockSpec((1, slots, t.shape[2]), lambda g: (g, 0, 0)) for t in trigs]
    return pl.pallas_call(
        functools.partial(forward_kernel, bands // 2, levels),
        out_shape=(
            jax.ShapeDtypeStruct((bands, rows, LANES), jnp.float32),
            jax.ShapeDtypeStruct((bands, 4, slots, cells), jnp.bfloat16),
        ),
        grid=(bands,),
        in_specs=per_slot + [whole],
        out_specs=(
            pl.BlockSpec((1, rows, LANES), lambda g: (g, 0, 0)),
            pl.BlockSpec((1, 4, slots, cells), lambda g: (g, 0, 0, 0)),
        ),
        scratch_shapes=[pltpu.VMEM((2, padded, cells), jnp.bfloat16)],
        name="forward",
    )(*trigs, field)


def hemi_kernel(slots, levels, rows, x_ref, o_ref):
    bands = x_ref.shape[0]
    half = bands // 2
    half_lat = half * rows
    wide = levels * rows
    tail = tail_of(wide)
    length = levels * half_lat
    source = lax.broadcasted_iota(jnp.int32, (LANES, length), 0)
    target = lax.broadcasted_iota(jnp.int32, (LANES, length), 1)
    sums = [None, None]
    for band in range(half):
        north = x_ref[band]
        south = x_ref[bands - 1 - band]
        main = placement(source, rows, half_lat, band, False)
        main = one_hot(jnp.logical_and(target == main, source < wide))
        ends = []
        if tail:
            groups = LANES // tail
            each = 2 * slots // groups
            for k in range(groups):
                cell = source - k * tail + LANES
                lane = placement(cell, rows, half_lat, band, False)
                inside = jnp.logical_and(source >= k * tail, source < (k + 1) * tail)
                ends.append(one_hot(jnp.logical_and(target == lane, inside)))
        for parity, value in enumerate((north + south, north - south)):
            term = dot_nn(value[: 2 * slots].astype(jnp.bfloat16), main)
            if tail:
                end = value[2 * slots :].astype(jnp.bfloat16)
                term = term + jnp.concatenate([dot_nn(end, place) for place in ends], axis=0)
            sums[parity] = term if band == 0 else sums[parity] + term
    for parity in range(2):
        o_ref[parity] = sums[parity].astype(jnp.bfloat16)


def hemispheres(x, slots, levels, rows):
    length = levels * rows * x.shape[0] // 2
    vmem = pl.BlockSpec(memory_space=pltpu.VMEM)
    return pl.pallas_call(
        functools.partial(hemi_kernel, slots, levels, rows),
        out_shape=jax.ShapeDtypeStruct((2, 2 * slots, length), jnp.bfloat16),
        in_specs=[vmem],
        out_specs=vmem,
        name="hemispheres",
    )(x)


def zonal_kernel(slots, levels, rows, x_ref, o_ref):
    bands = o_ref.shape[0]
    half = bands // 2
    half_lat = half * rows
    wide = levels * rows
    tail = tail_of(wide)
    length = levels * half_lat
    sides = (x_ref[0] + x_ref[1], x_ref[0] - x_ref[1])
    source = lax.broadcasted_iota(jnp.int32, (LANES, length), 0)
    target = lax.broadcasted_iota(jnp.int32, (LANES, length), 1)
    for side, value in enumerate(sides):
        flip = side == 1
        groups = LANES // tail if tail else 1
        each = 2 * slots // groups
        whole = value.astype(jnp.bfloat16)
        chunks = [value[k * each : (k + 1) * each].astype(jnp.bfloat16) for k in range(groups)]
        for band in range(half):
            slot = bands - 1 - band if flip else band
            main = placement(source, rows, half_lat, band, flip)
            main = one_hot(jnp.logical_and(target == main, source < wide))
            o_ref[slot, : 2 * slots, :] = dot_nt(whole, main).astype(jnp.bfloat16)
            if tail:
                total = None
                for k in range(groups):
                    cell = source - k * tail + LANES
                    lane = placement(cell, rows, half_lat, band, flip)
                    inside = jnp.logical_and(source >= k * tail, source < (k + 1) * tail)
                    term = dot_nt(chunks[k], one_hot(jnp.logical_and(target == lane, inside)))
                    total = term if k == 0 else total + term
                o_ref[slot, 2 * slots :, :] = total.astype(jnp.bfloat16)


def zonals(x, slots, levels, rows, bands):
    out_rows = packed_rows(slots, levels * rows)
    vmem = pl.BlockSpec(memory_space=pltpu.VMEM)
    return pl.pallas_call(
        functools.partial(zonal_kernel, slots, levels, rows),
        out_shape=jax.ShapeDtypeStruct((bands, out_rows, LANES), jnp.bfloat16),
        in_specs=[vmem],
        out_specs=vmem,
        name="zonals",
    )(x)


def inverse_kernel(weights, tables, x_ref, o_ref):
    wide = o_ref.shape[0]
    slots = tables.shape[2]
    tail = tail_of(wide)
    value = x_ref[0].astype(jnp.float32)
    main = value[: 2 * slots]
    pieces = [main]
    if tail:
        groups = LANES // tail
        end = value[2 * slots :]
        spread = [end] + [pltpu.roll(end, LANES - k * tail, 1) for k in range(1, groups)]
        pieces.append(jnp.concatenate(spread, axis=0))
    first = pl.program_id(0) == 0
    for number, piece in enumerate(pieces):
        term = None
        for part in range(2):
            weighted = piece[part * slots : (part + 1) * slots] * weights[0]
            turned = weighted.T.astype(jnp.bfloat16)
            for low in range(2):
                one = dot_nn(turned, tables[0, 2 * part + low])
                term = one if term is None else term + one
        begin = number * LANES
        count = min(LANES, wide - begin)
        place = slice(begin, begin + count)

        @pl.when(first)
        def _():
            o_ref[place, :] = term[:count]

        @pl.when(jnp.logical_not(first))
        def _():
            o_ref[place, :] += term[:count]


def inverse(x, weights, tables, wide):
    bands, rows, _ = x.shape
    slots, cells = tables.shape[2:]
    return pl.pallas_call(
        inverse_kernel,
        out_shape=jax.ShapeDtypeStruct((wide, cells), jnp.float32),
        grid=(bands,),
        in_specs=[
            pl.BlockSpec((1, slots, 1), lambda g: (g, 0, 0)),
            pl.BlockSpec((1, 4, slots, cells), lambda g: (g, 0, 0, 0)),
            pl.BlockSpec((1, rows, LANES), lambda g: (g, 0, 0)),
        ],
        out_specs=pl.BlockSpec((wide, cells), lambda g: (0, 0)),
        name="inverse",
    )(weights, tables, x)


def transport_kernel(stencil_ref, band_ref, up_ref, down_ref, code_ref, o_ref, ext, codes, rolled):
    levels, rows, cells = band_ref.shape
    tall = ext.shape[1]
    codes[...] = jnp.full(codes.shape, -1, jnp.int32)
    codes[0:rows, :] = code_ref[...]
    for level in range(levels):
        ext[level, tall - 8 : tall, :] = jnp.zeros((8, cells), jnp.float32)
        ext[level, 0:REACH, :] = up_ref[level]
        ext[level, REACH : REACH + rows, :] = band_ref[level]
        ext[level, REACH + rows : 2 * REACH + rows, :] = down_ref[level]
        for b in range(7):
            whole = ext[level]
            shift = (REACH - b) % cells
            rolled[b, level] = pltpu.roll(whole, shift, 1) if shift else whole

    @pl.loop(0, cells // LANES)
    def _(column):
        lanes = pl.ds(pl.multiple_of(column * LANES, LANES), LANES)
        code = codes[:, lanes]
        sums = [jnp.zeros((tall, LANES), jnp.float32) for _ in range(levels)]
        for a in range(7):
            code_a = pltpu.roll(code, a, 0) if a else code
            terms = [None] * levels
            for b in range(7):
                weight = stencil_ref[a, b]
                factor = jnp.where(code_a == a * 7 + b, weight + 1.0, weight)
                for level in range(levels):
                    term = factor * rolled[b, level, :, lanes]
                    terms[level] = term if b == 0 else terms[level] + term
            for level in range(levels):
                term = pltpu.roll(terms[level], tall - a, 0) if a else terms[level]
                sums[level] = sums[level] + term
        for level in range(levels):
            o_ref[level * rows : (level + 1) * rows, lanes] = sums[level][0:rows]


def transport(band, up, down, offsets, stencil):
    levels, rows, cells = band.shape
    tall = -(-(rows + 2 * REACH) // 8) * 8
    code = (offsets[0] + REACH) * 7 + offsets[1] + REACH
    vmem = pl.BlockSpec(memory_space=pltpu.VMEM)
    return pl.pallas_call(
        transport_kernel,
        out_shape=jax.ShapeDtypeStruct((levels * rows, cells), jnp.float32),
        in_specs=[pl.BlockSpec(memory_space=pltpu.SMEM), vmem, vmem, vmem, vmem],
        out_specs=vmem,
        scratch_shapes=[
            pltpu.VMEM((levels, tall, cells), jnp.float32),
            pltpu.VMEM((tall, cells), jnp.int32),
            pltpu.VMEM((7, levels, tall, cells), jnp.float32),
        ],
        name="transport",
    )(stencil, band, up, down, code)


def halo(cells, width):
    count = lax.axis_size("lat")
    ends = count - 1
    head = cells[:, :width]
    tail = cells[:, cells.shape[1] - width :]
    up = lax.ppermute(tail, "lat", [(i, i + 1) for i in range(ends)])
    down = lax.ppermute(head, "lat", [(i + 1, i) for i in range(ends)])
    return up, down


def trig(steps, assign, lon_cells):
    phase = assign[..., None] * steps % lon_cells
    angles = phase.astype(jnp.float32) * (2.0 * math.pi / lon_cells)
    return jnp.cos(angles), jnp.sin(angles)


def wave_trigs(assign, lon_cells):
    fine = jnp.arange(LANES, dtype=jnp.int32)
    coarse = jnp.arange(lon_cells // LANES, dtype=jnp.int32) * LANES
    c2, s2 = trig(fine, assign, lon_cells)
    c1, s1 = trig(coarse, assign, lon_cells)
    scale = 1.0 / math.sqrt(lon_cells)
    weights = jnp.where(assign == 0, 1.0, 2.0)
    weights = weights.astype(jnp.float32)[..., None]
    return (c1 * scale, s1 * scale, c2, s2), weights


def vertical(spectra, my_waves, first_degree, damping, vert_vecs, vert_inv):
    degree_span = spectra.shape[2]
    degrees = first_degree + jnp.arange(degree_span, dtype=jnp.int32)
    parity = jnp.arange(2, dtype=jnp.int32)
    degree_n = my_waves[:, None, None] + 2 * degrees[None, None, :] + parity[None, :, None]
    inside = (degree_n <= M - 1).astype(jnp.float32)
    forcing = spectra * inside[:, :, :, None, None]
    modal = jnp.einsum("kq,rpicq->rpick", vert_inv, forcing, precision=EXACT)
    scaled_n = degree_n.astype(jnp.float32)
    growth = scaled_n * (scaled_n + 1.0) / float(M * M)
    denominator = 1.0 + growth[:, :, :, None, None] * damping[None, None, None, None, :]
    modal = modal / denominator
    return jnp.einsum("kq,rpicq->rpick", vert_vecs, modal, precision=EXACT)


def on_device(tracer, offsets, stencil, assign, legendre, damping, vert_vecs, vert_inv):
    levels, rows, lon_cells = tracer.shape
    bands = lax.axis_size("lat")
    planes = lax.axis_size("lev")
    slots = legendre.shape[0]
    half = bands // 2
    half_lat = half * rows
    me = lax.axis_index("lat")
    up, down = halo(tracer, REACH)
    trigs, weights = wave_trigs(assign.reshape(bands, slots), lon_cells)
    advected = transport(tracer, up, down, offsets, stencil)
    sent, tables = forward(advected, levels, trigs, bands, slots)
    got = exchange(sent, "lat", 1)
    hemi = gather(hemispheres(got, slots, levels, rows), "lev", 2)
    hemi = hemi.reshape(planes, 2, 2, slots, levels, half_lat)
    hemi = hemi.transpose(3, 1, 2, 0, 4, 5).reshape(slots, 2, 2, planes * levels, half_lat)

    my_waves = lax.dynamic_slice_in_dim(assign, me * slots, slots)
    first_degree = lax.axis_index("lev") * legendre.shape[2]
    spectra = jnp.einsum(
        "rpij,rpclj->rpicl", legendre, hemi, preferred_element_type=jnp.float32
    )
    solved = vertical(spectra, my_waves, first_degree, damping, vert_vecs, vert_inv)
    packed = solved.astype(jnp.bfloat16)
    back = jnp.einsum(
        "rpij,rpicl->rpclj", legendre, packed, preferred_element_type=jnp.float32
    )
    back = back.astype(jnp.bfloat16).reshape(slots, 2, 2, planes, levels, half_lat)
    back = back.transpose(3, 1, 2, 0, 4, 5).reshape(planes, 2, 2 * slots, levels * half_lat)
    total = scatter(back, "lev", 3)
    waves = exchange(zonals(total, slots, levels, rows, bands), "lat", 4)
    tracer_new = inverse(waves, weights, tables, levels * rows)
    tracer_new = tracer_new.reshape(levels, rows, lon_cells)
    spectral_new = solved.reshape(slots, 2, solved.shape[2], -1)
    return (tracer_new, spectral_new)


def solution(mesh):
    in_specs = (
        P("lev", "lat", None),
        P(None, "lat", None),
        P(),
        P(),
        P("lat", None, "lev", None),
        P(),
        P(),
        P(),
    )
    out_specs = (P("lev", "lat", None), P("lat", None, "lev", None))
    return jax.shard_map(
        on_device, mesh=mesh, in_specs=in_specs, out_specs=out_specs, check_vma=False
    )
```

```python
import functools
import math

import jax
import jax.numpy as jnp
from jax import lax
from jax.experimental import pallas as pl
from jax.experimental.pallas import tpu as pltpu
from jax.sharding import PartitionSpec as P

M = 640
LANES = 128
REACH = 3

EXACT = lax.Precision.HIGHEST


def exchange_kernel(axis, count, spread, x_ref, o_ref, send_sems, recv_sems, own_sem):
    me = lax.axis_index(axis)
    barrier = pltpu.get_barrier_semaphore()
    for step in range(1, count):
        peer = lax.rem(me + step, count)
        pl.semaphore_signal(
            barrier, inc=1, device_id={axis: peer}, device_id_type=pl.DeviceIdType.MESH
        )
    pl.semaphore_wait(barrier, count - 1)
    copies = []
    for step in range(1, count):
        peer = lax.rem(me + step, count)
        copy = pltpu.make_async_remote_copy(
            src_ref=x_ref.at[peer] if spread else x_ref,
            dst_ref=o_ref.at[me],
            send_sem=send_sems.at[step - 1],
            recv_sem=recv_sems.at[step - 1],
            device_id={axis: peer},
            device_id_type=pl.DeviceIdType.MESH,
        )
        copy.start()
        copies.append(copy)
    own = pltpu.make_async_copy(x_ref.at[me] if spread else x_ref, o_ref.at[me], own_sem)
    own.start()
    own.wait()
    for copy in copies:
        copy.wait()


def exchange(x, axis, collective_id, spread=True):
    count = lax.axis_size(axis)
    block = x.shape[1:] if spread else x.shape
    return pl.pallas_call(
        functools.partial(exchange_kernel, axis, count, spread),
        out_shape=jax.ShapeDtypeStruct((count,) + block, x.dtype),
        in_specs=[pl.BlockSpec(memory_space=pltpu.VMEM)],
        out_specs=pl.BlockSpec(memory_space=pltpu.VMEM),
        scratch_shapes=[
            pltpu.SemaphoreType.DMA((count - 1,)),
            pltpu.SemaphoreType.DMA((count - 1,)),
            pltpu.SemaphoreType.DMA,
        ],
        compiler_params=pltpu.CompilerParams(
            collective_id=collective_id, has_side_effects=True
        ),
        name="exchange_%d" % collective_id,
    )(x)


def greet_neighbours(axis, count, me):
    barrier = pltpu.get_barrier_semaphore()
    ways = ((me > 0, me - 1), (me < count - 1, me + 1))
    for there, peer in ways:

        @pl.when(there)
        def _():
            pl.semaphore_signal(
                barrier, inc=1, device_id={axis: peer}, device_id_type=pl.DeviceIdType.MESH
            )

    inner = jnp.logical_and(me > 0, me < count - 1)

    @pl.when(inner)
    def _():
        pl.semaphore_wait(barrier, 2)

    @pl.when(jnp.logical_not(inner))
    def _():
        pl.semaphore_wait(barrier, 1)


def scatter_kernel(axis, count, x_ref, o_ref, land, outs, send_sems, recv_sems):
    me = lax.axis_index(axis)
    greet_neighbours(axis, count, me)
    fed_from = (me < count - 1, me > 0)
    parities = x_ref.shape[1]

    def leg(way, dest, source, target):
        return pltpu.make_async_remote_copy(
            src_ref=source,
            dst_ref=land.at[way, dest],
            send_sem=send_sems.at[way, dest],
            recv_sem=recv_sems.at[way, dest],
            device_id={axis: target},
            device_id_type=pl.DeviceIdType.MESH,
        )

    legs = []
    for k in range(count - 1):
        for way in range(2):
            dest = k if way == 0 else count - 1 - k
            away = me > dest if way == 0 else me < dest
            target = me - 1 if way == 0 else me + 1
            legs.append((way, dest, away, target))

            @pl.when(jnp.logical_and(away, jnp.logical_not(fed_from[way])))
            def _():
                leg(way, dest, x_ref.at[dest], target).start()

            @pl.when(jnp.logical_and(away, fed_from[way]))
            def _():
                leg(way, dest, x_ref.at[dest], target).wait_recv()

                @pl.loop(0, parities)
                def _(parity):
                    total = land[way, dest, parity].astype(jnp.float32)
                    total = total + x_ref[dest, parity].astype(jnp.float32)
                    outs[way, dest, parity] = total.astype(outs.dtype)

                leg(way, dest, outs.at[way, dest], target).start()

    @pl.loop(0, parities)
    def _(parity):
        o_ref[parity] = x_ref[me, parity].astype(jnp.float32)

    for way in range(2):

        @pl.when(fed_from[way])
        def _():
            leg(way, me, x_ref.at[me], lax.rem(me + 1, count)).wait_recv()

            @pl.loop(0, parities)
            def _(parity):
                o_ref[parity] += land[way, me, parity].astype(jnp.float32)

    for way, dest, away, target in legs:

        @pl.when(away)
        def _():
            leg(way, dest, outs.at[way, dest], target).wait_send()


def scatter(x, axis, collective_id):
    count = lax.axis_size(axis)
    vmem = pl.BlockSpec(memory_space=pltpu.VMEM)
    return pl.pallas_call(
        functools.partial(scatter_kernel, axis, count),
        out_shape=jax.ShapeDtypeStruct(x.shape[1:], jnp.float32),
        in_specs=[vmem],
        out_specs=vmem,
        scratch_shapes=[
            pltpu.VMEM((2,) + x.shape, x.dtype),
            pltpu.VMEM((2,) + x.shape, x.dtype),
            pltpu.SemaphoreType.DMA((2, count)),
            pltpu.SemaphoreType.DMA((2, count)),
        ],
        compiler_params=pltpu.CompilerParams(
            collective_id=collective_id, has_side_effects=True
        ),
        name="scatter_%d" % collective_id,
    )(x)


def tail_of(wide):
    tail = max(wide - LANES, 0)
    assert tail == 0 or LANES % tail == 0
    return tail


def packed_rows(slots, wide):
    tail = tail_of(wide)
    return 2 * slots + (2 * slots * tail) // LANES


def placement(source, rows, half_lat, band, flip):
    level = jnp.zeros_like(source)
    for k in range(1, 2 + (LANES * 2) // rows):
        level = level + (source >= k * rows).astype(jnp.int32)
    row = source - level * rows
    if flip:
        row = rows - 1 - row
    return level * half_lat + band * rows + row


def one_hot(pick):
    return jnp.where(pick, 1.0, 0.0).astype(jnp.bfloat16)


def split(x):
    high = x.astype(jnp.bfloat16)
    return high, (x - high.astype(jnp.float32)).astype(jnp.bfloat16)


def dot_nt(a, b):
    return lax.dot_general(a, b, (((1,), (1,)), ((), ())), preferred_element_type=jnp.float32)


def dot_nn(a, b):
    return jnp.dot(a, b, preferred_element_type=jnp.float32)


def fill_tables(c1, s1, c2, s2, tables):
    fine_c, fine_s = c2[0], s2[0]
    for a in range(c1.shape[2]):
        lanes = slice(a * LANES, (a + 1) * LANES)
        coarse_c, coarse_s = c1[0, :, a : a + 1], s1[0, :, a : a + 1]
        cosines = coarse_c * fine_c - coarse_s * fine_s
        sines = -(coarse_s * fine_c + coarse_c * fine_s)
        for part, values in enumerate((cosines, sines)):
            high, low = split(values)
            tables[0, 2 * part, :, lanes] = high
            tables[0, 2 * part + 1, :, lanes] = low


def forward_kernel(half, levels, c1, s1, c2, s2, field, o_ref, tables, cells):
    wide = field.shape[0]
    rows = wide // levels
    slots = c1.shape[1]
    padded = cells.shape[1]
    tail = tail_of(wide)
    southern = lax.axis_index("lat") >= half

    @pl.when(pl.program_id(0) == 0)
    def _():
        to = lax.broadcasted_iota(jnp.int32, (padded, wide), 0)
        origin = lax.broadcasted_iota(jnp.int32, (padded, wide), 1)
        level = jnp.zeros_like(to)
        for k in range(1, levels):
            level = level + (to >= k * rows).astype(jnp.int32)
        mirrored = 2 * level * rows + rows - 1 - to
        wanted = jnp.where(southern, mirrored, to)
        pick = one_hot(jnp.logical_and(origin == wanted, to < wide))
        high, low = split(field[...])
        cells[0] = dot_nn(pick, high).astype(jnp.bfloat16)
        cells[1] = dot_nn(pick, low).astype(jnp.bfloat16)

    fill_tables(c1, s1, c2, s2, tables)
    tails = []
    for part in range(2):
        found = (
            dot_nt(tables[0, 2 * part], cells[0])
            + dot_nt(tables[0, 2 * part], cells[1])
            + dot_nt(tables[0, 2 * part + 1], cells[0])
        )
        o_ref[0, part * slots : (part + 1) * slots, :] = found[:, :LANES]
        if tail:
            tails.append(found[:, LANES:])
    if tail:
        groups = LANES // tail
        each = 2 * slots // groups
        both = jnp.concatenate(tails, axis=0)
        total = both[:each]
        for k in range(1, groups):
            total = total + pltpu.roll(both[k * each : (k + 1) * each], k * tail, 1)
        o_ref[0, 2 * slots :, :] = total


def forward(field, levels, trigs, bands, slots):
    wide, cells = field.shape
    padded = LANES * (1 if wide <= LANES else 2)
    rows = packed_rows(slots, wide)
    whole = pl.BlockSpec(field.shape, lambda g: (0, 0))
    per_slot = [pl.BlockSpec((1, slots, t.shape[2]), lambda g: (g, 0, 0)) for t in trigs]
    return pl.pallas_call(
        functools.partial(forward_kernel, bands // 2, levels),
        out_shape=(
            jax.ShapeDtypeStruct((bands, rows, LANES), jnp.float32),
            jax.ShapeDtypeStruct((bands, 4, slots, cells), jnp.bfloat16),
        ),
        grid=(bands,),
        in_specs=per_slot + [whole],
        out_specs=(
            pl.BlockSpec((1, rows, LANES), lambda g: (g, 0, 0)),
            pl.BlockSpec((1, 4, slots, cells), lambda g: (g, 0, 0, 0)),
        ),
        scratch_shapes=[pltpu.VMEM((2, padded, cells), jnp.bfloat16)],
        name="forward",
    )(*trigs, field)


def hemi_kernel(slots, levels, rows, x_ref, o_ref):
    bands = x_ref.shape[0]
    half = bands // 2
    half_lat = half * rows
    wide = levels * rows
    tail = tail_of(wide)
    length = levels * half_lat
    source = lax.broadcasted_iota(jnp.int32, (LANES, length), 0)
    target = lax.broadcasted_iota(jnp.int32, (LANES, length), 1)
    sums = [None, None]
    for band in range(half):
        north = x_ref[band]
        south = x_ref[bands - 1 - band]
        main = placement(source, rows, half_lat, band, False)
        main = one_hot(jnp.logical_and(target == main, source < wide))
        ends = []
        if tail:
            groups = LANES // tail
            each = 2 * slots // groups
            for k in range(groups):
                cell = source - k * tail + LANES
                lane = placement(cell, rows, half_lat, band, False)
                inside = jnp.logical_and(source >= k * tail, source < (k + 1) * tail)
                ends.append(one_hot(jnp.logical_and(target == lane, inside)))
        for parity, value in enumerate((north + south, north - south)):
            term = dot_nn(value[: 2 * slots].astype(jnp.bfloat16), main)
            if tail:
                end = value[2 * slots :].astype(jnp.bfloat16)
                term = term + jnp.concatenate([dot_nn(end, place) for place in ends], axis=0)
            sums[parity] = term if band == 0 else sums[parity] + term
    for parity in range(2):
        o_ref[parity] = sums[parity].astype(jnp.bfloat16)


def hemispheres(x, slots, levels, rows):
    length = levels * rows * x.shape[0] // 2
    vmem = pl.BlockSpec(memory_space=pltpu.VMEM)
    return pl.pallas_call(
        functools.partial(hemi_kernel, slots, levels, rows),
        out_shape=jax.ShapeDtypeStruct((2, 2 * slots, length), jnp.bfloat16),
        in_specs=[vmem],
        out_specs=vmem,
        name="hemispheres",
    )(x)


def zonal_kernel(slots, levels, rows, x_ref, o_ref):
    bands = o_ref.shape[0]
    half = bands // 2
    half_lat = half * rows
    wide = levels * rows
    tail = tail_of(wide)
    length = levels * half_lat
    sides = (x_ref[0] + x_ref[1], x_ref[0] - x_ref[1])
    source = lax.broadcasted_iota(jnp.int32, (LANES, length), 0)
    target = lax.broadcasted_iota(jnp.int32, (LANES, length), 1)
    for side, value in enumerate(sides):
        flip = side == 1
        groups = LANES // tail if tail else 1
        each = 2 * slots // groups
        whole = value.astype(jnp.bfloat16)
        chunks = [value[k * each : (k + 1) * each].astype(jnp.bfloat16) for k in range(groups)]
        for band in range(half):
            slot = bands - 1 - band if flip else band
            main = placement(source, rows, half_lat, band, flip)
            main = one_hot(jnp.logical_and(target == main, source < wide))
            o_ref[slot, : 2 * slots, :] = dot_nt(whole, main).astype(jnp.bfloat16)
            if tail:
                total = None
                for k in range(groups):
                    cell = source - k * tail + LANES
                    lane = placement(cell, rows, half_lat, band, flip)
                    inside = jnp.logical_and(source >= k * tail, source < (k + 1) * tail)
                    term = dot_nt(chunks[k], one_hot(jnp.logical_and(target == lane, inside)))
                    total = term if k == 0 else total + term
                o_ref[slot, 2 * slots :, :] = total.astype(jnp.bfloat16)


def zonals(x, slots, levels, rows, bands):
    out_rows = packed_rows(slots, levels * rows)
    vmem = pl.BlockSpec(memory_space=pltpu.VMEM)
    return pl.pallas_call(
        functools.partial(zonal_kernel, slots, levels, rows),
        out_shape=jax.ShapeDtypeStruct((bands, out_rows, LANES), jnp.bfloat16),
        in_specs=[vmem],
        out_specs=vmem,
        name="zonals",
    )(x)


def inverse_kernel(weights, tables, x_ref, o_ref):
    wide = o_ref.shape[0]
    slots = tables.shape[2]
    tail = tail_of(wide)
    value = x_ref[0].astype(jnp.float32)
    both = value[: 2 * slots]
    if tail:
        groups = LANES // tail
        end = value[2 * slots :]
        spread = [end] + [pltpu.roll(end, LANES - k * tail, 1) for k in range(1, groups)]
        both = jnp.concatenate([both, jnp.concatenate(spread, axis=0)], axis=1)
    term = None
    for part in range(2):
        weighted = both[part * slots : (part + 1) * slots] * weights[0]
        turned = weighted.T[:wide].astype(jnp.bfloat16)
        for low in range(2):
            one = dot_nn(turned, tables[0, 2 * part + low])
            term = one if term is None else term + one
    first = pl.program_id(0) == 0

    @pl.when(first)
    def _():
        o_ref[...] = term

    @pl.when(jnp.logical_not(first))
    def _():
        o_ref[...] += term


def inverse(x, weights, tables, wide):
    bands, rows, _ = x.shape
    slots, cells = tables.shape[2:]
    return pl.pallas_call(
        inverse_kernel,
        out_shape=jax.ShapeDtypeStruct((wide, cells), jnp.float32),
        grid=(bands,),
        in_specs=[
            pl.BlockSpec((1, slots, 1), lambda g: (g, 0, 0)),
            pl.BlockSpec((1, 4, slots, cells), lambda g: (g, 0, 0, 0)),
            pl.BlockSpec((1, rows, LANES), lambda g: (g, 0, 0)),
        ],
        out_specs=pl.BlockSpec((wide, cells), lambda g: (0, 0)),
        name="inverse",
    )(weights, tables, x)


def transport_kernel(stencil_ref, band_ref, up_ref, down_ref, code_ref, o_ref, ext, codes, rolled):
    levels, rows, cells = band_ref.shape
    tall = ext.shape[1]
    codes[...] = jnp.full(codes.shape, -1, jnp.int32)
    codes[0:rows, :] = code_ref[...]
    for level in range(levels):
        ext[level, tall - 8 : tall, :] = jnp.zeros((8, cells), jnp.float32)
        ext[level, 0:REACH, :] = up_ref[level]
        ext[level, REACH : REACH + rows, :] = band_ref[level]
        ext[level, REACH + rows : 2 * REACH + rows, :] = down_ref[level]
        for b in range(7):
            whole = ext[level]
            shift = (REACH - b) % cells
            rolled[b, level] = pltpu.roll(whole, shift, 1) if shift else whole

    @pl.loop(0, cells // LANES)
    def _(column):
        lanes = pl.ds(pl.multiple_of(column * LANES, LANES), LANES)
        code = codes[:, lanes]
        sums = [jnp.zeros((tall, LANES), jnp.float32) for _ in range(levels)]
        for a in range(7):
            code_a = pltpu.roll(code, a, 0) if a else code
            terms = [None] * levels
            for b in range(7):
                weight = stencil_ref[a, b]
                factor = jnp.where(code_a == a * 7 + b, weight + 1.0, weight)
                for level in range(levels):
                    term = factor * rolled[b, level, :, lanes]
                    terms[level] = term if b == 0 else terms[level] + term
            for level in range(levels):
                term = pltpu.roll(terms[level], tall - a, 0) if a else terms[level]
                sums[level] = sums[level] + term
        for level in range(levels):
            o_ref[level * rows : (level + 1) * rows, lanes] = sums[level][0:rows]


def transport(band, up, down, offsets, stencil):
    levels, rows, cells = band.shape
    tall = -(-(rows + 2 * REACH) // 8) * 8
    code = (offsets[0] + REACH) * 7 + offsets[1] + REACH
    vmem = pl.BlockSpec(memory_space=pltpu.VMEM)
    return pl.pallas_call(
        transport_kernel,
        out_shape=jax.ShapeDtypeStruct((levels * rows, cells), jnp.float32),
        in_specs=[pl.BlockSpec(memory_space=pltpu.SMEM), vmem, vmem, vmem, vmem],
        out_specs=vmem,
        scratch_shapes=[
            pltpu.VMEM((levels, tall, cells), jnp.float32),
            pltpu.VMEM((tall, cells), jnp.int32),
            pltpu.VMEM((7, levels, tall, cells), jnp.float32),
        ],
        name="transport",
    )(stencil, band, up, down, code)


def halo(cells, width):
    count = lax.axis_size("lat")
    ends = count - 1
    head = cells[:, :width]
    tail = cells[:, cells.shape[1] - width :]
    up = lax.ppermute(tail, "lat", [(i, i + 1) for i in range(ends)])
    down = lax.ppermute(head, "lat", [(i + 1, i) for i in range(ends)])
    return up, down


def trig(steps, assign, lon_cells):
    phase = assign[..., None] * steps % lon_cells
    angles = phase.astype(jnp.float32) * (2.0 * math.pi / lon_cells)
    return jnp.cos(angles), jnp.sin(angles)


def wave_trigs(assign, lon_cells):
    fine = jnp.arange(LANES, dtype=jnp.int32)
    coarse = jnp.arange(lon_cells // LANES, dtype=jnp.int32) * LANES
    c2, s2 = trig(fine, assign, lon_cells)
    c1, s1 = trig(coarse, assign, lon_cells)
    scale = 1.0 / math.sqrt(lon_cells)
    weights = jnp.where(assign == 0, 1.0, 2.0)
    weights = weights.astype(jnp.float32)[..., None]
    return (c1 * scale, s1 * scale, c2, s2), weights


def vertical(spectra, my_waves, first_degree, damping, vert_vecs, vert_inv):
    degree_span = spectra.shape[2]
    degrees = first_degree + jnp.arange(degree_span, dtype=jnp.int32)
    parity = jnp.arange(2, dtype=jnp.int32)
    degree_n = my_waves[:, None, None] + 2 * degrees[None, None, :] + parity[None, :, None]
    inside = (degree_n <= M - 1).astype(jnp.float32)
    forcing = spectra * inside[:, :, :, None, None]
    modal = jnp.einsum("kq,rpicq->rpick", vert_inv, forcing, precision=EXACT)
    scaled_n = degree_n.astype(jnp.float32)
    growth = scaled_n * (scaled_n + 1.0) / float(M * M)
    denominator = 1.0 + growth[:, :, :, None, None] * damping[None, None, None, None, :]
    modal = modal / denominator
    return jnp.einsum("kq,rpicq->rpick", vert_vecs, modal, precision=EXACT)


def on_device(tracer, offsets, stencil, assign, legendre, damping, vert_vecs, vert_inv):
    levels, rows, lon_cells = tracer.shape
    bands = lax.axis_size("lat")
    planes = lax.axis_size("lev")
    slots = legendre.shape[0]
    half = bands // 2
    half_lat = half * rows
    me = lax.axis_index("lat")
    up, down = halo(tracer, REACH)
    trigs, weights = wave_trigs(assign.reshape(bands, slots), lon_cells)
    advected = transport(tracer, up, down, offsets, stencil)
    sent, tables = forward(advected, levels, trigs, bands, slots)
    got = exchange(sent, "lat", 1)
    hemi = exchange(hemispheres(got, slots, levels, rows), "lev", 2, spread=False)
    hemi = hemi.reshape(planes, 2, 2, slots, levels, half_lat)
    hemi = hemi.transpose(3, 1, 2, 0, 4, 5).reshape(slots, 2, 2, planes * levels, half_lat)

    my_waves = lax.dynamic_slice_in_dim(assign, me * slots, slots)
    first_degree = lax.axis_index("lev") * legendre.shape[2]
    spectra = jnp.einsum(
        "rpij,rpclj->rpicl", legendre, hemi, preferred_element_type=jnp.float32
    )
    solved = vertical(spectra, my_waves, first_degree, damping, vert_vecs, vert_inv)
    packed = solved.astype(jnp.bfloat16)
    back = jnp.einsum(
        "rpij,rpicl->rpclj", legendre, packed, preferred_element_type=jnp.float32
    )
    back = back.astype(jnp.bfloat16).reshape(slots, 2, 2, planes, levels, half_lat)
    back = back.transpose(3, 1, 2, 0, 4, 5).reshape(planes, 2, 2 * slots, levels * half_lat)
    total = scatter(back, "lev", 3)
    waves = exchange(zonals(total, slots, levels, rows, bands), "lat", 4)
    tracer_new = inverse(waves, weights, tables, levels * rows)
    tracer_new = tracer_new.reshape(levels, rows, lon_cells)
    spectral_new = solved.reshape(slots, 2, solved.shape[2], -1)
    return (tracer_new, spectral_new)


def solution(mesh):
    in_specs = (
        P("lev", "lat", None),
        P(None, "lat", None),
        P(),
        P(),
        P("lat", None, "lev", None),
        P(),
        P(),
        P(),
    )
    out_specs = (P("lev", "lat", None), P("lat", None, "lev", None))
    return jax.shard_map(
        on_device, mesh=mesh, in_specs=in_specs, out_specs=out_specs, check_vma=False
    )
```
